128 devices in a mesh: hist: 8 (over z_hi, x), tcol: 16 (over z_lo, y, core).
Axes of the slice: x: 4, y: 4, z: 4 (z_hi: 2, z_lo: 2; z = z_hi * 2 + z_lo), core: 2. Of those that a mesh axis runs over, the one named last changes fastest.
Arguments:
- history: float32 [16384, 8192], P('hist', 'tcol'), may hold values from -5 to 5
- memory_weight_first: float32 [512, 16384], P(None, 'hist'), may hold values from -0.0625 to 0.0625
- memory_weight_second: float32 [512, 16384], P(None, 'hist'), may hold values from -0.0625 to 0.0625
- link: float32 [512, 512], replicated, may hold values from -0.25 to 0.25
- propagator: float32 [8192, 8192], P(None, 'tcol'), may hold values from -0.0625 to 0.0625
- inverse_one: float32 [512, 512], replicated, as said below
- inverse_two: float32 [512, 512], replicated, as said below
- explicit_first: float32 [512, 8192], P(None, 'tcol'), may hold values from -5 to 5
- explicit_second: float32 [512, 8192], P(None, 'tcol'), may hold values from -5 to 5
Outputs:
- first_slab_rows: float32 [512, 8192], P('hist', 'tcol')
- slab_two: float32 [512, 8192], P('hist', 'tcol')
The draws below stay inside these ranges and needn't reach their ends.
Inputs may be any that keep to these rules, and one draw needn't show every extreme that they name: `inverse_one`: the identity plus independent entries of deviation 0.5 / sqrt(512). `inverse_two`: the identity plus independent entries of deviation 0.5 / sqrt(512).
All inputs are finite; a program needn't handle non-finite values.
Results may differ from the reference program's by a relative error of at most 0.0003.
Values sent between devices are 32-bit elements; how exact they have to be, the bound alone decides.
No kernel may reach another device: no remote copies, remote signals or barrier semaphores. Data moves between devices by JAX's collectives and lax.ppermute only.
A program may use at most 128 MiB of HBM per device.

```python
import jax
import jax.numpy as jnp
from jax import lax

S = 512
HT = 16384
NC = 8192


def inverse_common(key, salt):
    sub = jax.random.fold_in(key, salt)
    noise = jax.random.normal(sub, (S, S), jnp.float32)
    return jnp.eye(S, dtype=jnp.float32) + noise * (0.5 / jnp.sqrt(jnp.float32(S)))


def draw_inverse_one(key, part):
    return inverse_common(key, 101)


def draw_inverse_two(key, part):
    return inverse_common(key, 202)


def strengthened(values, stream_key, source, target, parts, factor):
    owner, partner = [(jnp.arange(values.shape[position]) // (values.shape[position] // parts)).reshape([-1 if axis == position else 1 for axis in range(values.ndim)]) for position in (source, target)]
    chosen = jax.random.permutation(stream_key, parts)[partner]
    strong = (owner == chosen) | (owner == (partner + parts // 2) % parts)
    return jnp.where(strong, factor * values, values)


def levels(own_key, extent, split, low, high):
    def one(position, shards_of):
        draws = jax.random.uniform(jax.random.fold_in(jax.random.fold_in(own_key, 6), position), (shards_of,), jnp.float32, low / len(split), high / len(split))
        return jnp.repeat(jnp.exp(draws), extent[position] // shards_of).reshape((-1,) + (1,) * (len(extent) - position - 1))

    loudness = one(*split[0])
    for cut in split[1:]:
        loudness = loudness * one(*cut)
    return loudness


def gaussian(rng, shape, deviation, limit, pieces=(), held_as=jnp.bfloat16):
    level = levels(rng, shape, pieces, -0.22, 0.18) if pieces else 1.0
    drawn = jax.random.normal(rng, shape, jnp.float32) * deviation * level
    return jnp.minimum(jnp.maximum(drawn, -limit), limit).astype(held_as)


def heavy_noise(key, shape, spread, reach, cuts, heavy, kind=jnp.bfloat16):
    result = spread * jax.random.normal(key, shape, jnp.float32)
    if cuts:
        result = result * levels(key, shape, cuts, -0.22, 0.18)
    return jnp.clip(strengthened(result, jax.random.fold_in(key, 3), *heavy), -reach, reach).astype(kind)


def setup_inputs(seed: int = 0) -> dict:
    key_list = jax.random.split(jax.random.key(seed), 10)
    return {
        "history": gaussian(key_list[0], (HT, NC), 0.8, 5.0, ((0, 8), (1, 16)), jnp.float32),
        "memory_weight_first": heavy_noise(key_list[1], (S, HT), HT ** -0.5, 0.0625, ((1, 8),), (1, 0, 8, 2.0), jnp.float32),
        "memory_weight_second": heavy_noise(key_list[2], (S, HT), HT ** -0.5, 0.0625, ((1, 8),), (1, 0, 8, 2.0), jnp.float32),
        "link": gaussian(key_list[3], (S, S), S ** -0.5, 0.25, (), jnp.float32),
        "propagator": gaussian(key_list[4], (NC, NC), NC ** -0.5, 0.0625, ((1, 16),), jnp.float32),
        "inverse_one": draw_inverse_one(jax.random.fold_in(key_list[9], 71), 0),
        "inverse_two": draw_inverse_two(jax.random.fold_in(key_list[9], 71), 0),
        "explicit_first": gaussian(key_list[7], (S, NC), 0.7, 5.0, ((1, 16),), jnp.float32),
        "explicit_second": gaussian(key_list[8], (S, NC), 0.7, 5.0, ((1, 16),), jnp.float32),
    }


strength = 0.2
step_size = 0.5
highest = lax.Precision.HIGHEST


def cubic_power(value):
    return strength * value * value * value


def matrix_product(left, right):
    return jnp.dot(left, right, preferred_element_type=jnp.float32, precision=highest)


def reference(history, memory_weight_first, memory_weight_second, link, propagator, inverse_one, inverse_two, explicit_first, explicit_second):
    self_energy_history = cubic_power(history)
    predictor_first = explicit_first + matrix_product(memory_weight_first, self_energy_history)
    mem_one = matrix_product(cubic_power(predictor_first), propagator)
    first_slab_rows = matrix_product(inverse_one, predictor_first + step_size * mem_one)
    collision_second = matrix_product(memory_weight_second, self_energy_history) + matrix_product(link, cubic_power(first_slab_rows))
    predictor_second = explicit_second + collision_second
    mem_two = matrix_product(cubic_power(predictor_second), propagator)
    slab_two = matrix_product(inverse_two, predictor_second + step_size * mem_two)
    return first_slab_rows, slab_two
```

```python
import jax
import jax.numpy as jnp
from jax import lax
from jax.experimental import pallas as pl
from jax.experimental.pallas import tpu as pltpu
from jax.sharding import PartitionSpec as P

strength = 0.2
step_size = 0.5
F32, BF16 = jnp.float32, jnp.bfloat16
WHOLE = pl.BlockSpec(memory_space=pltpu.VMEM)
SCALARS = pl.BlockSpec(memory_space=pltpu.SMEM)
UNREAD = pl.BlockSpec(memory_space=pl.ANY)

CHIPS = ((0, 0), (1, 2), (1, 1), (1, 3), (0, 2), (1, 0), (0, 1), (0, 3))


def move_hist(value, dz, dx):
    pairs = [(i, ((i >> 2) ^ dz) * 4 + ((i & 3) + dx) % 4) for i in range(8)]
    return lax.ppermute(value, "hist", pairs)


def move_tcol(value, dz, dy):
    pairs = [
        (i, ((i >> 3) ^ dz) * 8 + ((((i >> 1) & 3) + dy) % 4) * 2 + (i & 1)) for i in range(16)
    ]
    return lax.ppermute(value, "tcol", pairs)


def other_core(value):
    return lax.ppermute(value, "tcol", [(i, i ^ 1) for i in range(16)])


def cubic_power(value):
    return strength * value * value * value


def split(value):
    high = value.astype(BF16)
    return high, (value - high.astype(F32)).astype(BF16)


def product(left, right):
    def dot(a, b):
        return jnp.dot(a, b, preferred_element_type=F32)

    return dot(left[0], right[0]) + (dot(left[0], right[1]) + dot(left[1], right[0]))


def total(refs):
    value = refs[0][...]
    for ref in refs[1:]:
        value = value + ref[...]
    return value


def rows_from(start, count):
    return pl.ds(pl.multiple_of(start, count), count)


def call(kernel, outs, name, where, inputs, after=(), scratch=()):
    n = len(after)

    def body(at, *refs):
        kernel(at, *refs[: len(inputs)], *refs[len(inputs) + n :])

    return pl.pallas_call(
        body,
        in_specs=[SCALARS] + [WHOLE] * len(inputs) + [UNREAD] * n,
        out_shape=[jax.ShapeDtypeStruct(shape, dtype) for shape, dtype in outs],
        out_specs=[WHOLE] * len(outs),
        scratch_shapes=[pltpu.VMEM(shape, F32) for shape in scratch],
        name=name,
        compiler_params=pltpu.CompilerParams(vmem_limit_bytes=8 << 20),
    )(where, *inputs, *after)


def in_hbm(array):
    return pltpu.with_memory_space_constraint(array, pltpu.HBM)


def collect(history, weights, where, joined, after=()):
    depth, cols = history.shape
    rows = weights.shape[0]
    chunk = 256
    part = cols // 8
    n = len(after)

    def kernel(at, hist_ref, weight_ref, *rest):
        outs, acc, turned = rest[n:-2], rest[-2], rest[-1]
        step = pl.program_id(0)

        @pl.when(step == 0)
        def _():
            acc[...] = jnp.zeros_like(acc)

        acc[...] += product(split(weight_ref[...]), split(cubic_power(hist_ref[...])))

        @pl.when(step == pl.num_programs(0) - 1)
        def _():
            turned[...] = acc[...].T
            for near in range(2):
                for d in range(4):
                    member = (at[0] ^ (1 - near)) * 4 + ((at[1] + d) & 3)
                    block = turned[rows_from(member * part, part), :]
                    if joined:
                        outs[d][near] = block
                    else:
                        outs[near * 4 + d][...] = block

    shape = (2, part, rows) if joined else (part, rows)
    count = 4 if joined else 8
    return pl.pallas_call(
        kernel,
        grid_spec=pltpu.PrefetchScalarGridSpec(
            num_scalar_prefetch=1,
            grid=(depth // chunk,),
            in_specs=[
                pl.BlockSpec((chunk, cols), lambda r, at: (r, 0)),
                pl.BlockSpec((rows, chunk), lambda r, at: (0, r)),
            ]
            + [UNREAD] * n,
            out_specs=[WHOLE] * count,
            scratch_shapes=[pltpu.VMEM((rows, cols), F32), pltpu.VMEM((cols, rows), F32)],
        ),
        out_shape=[jax.ShapeDtypeStruct(shape, F32)] * count,
        name="collect",
        compiler_params=pltpu.CompilerParams(vmem_limit_bytes=12 << 20),
    )(where, in_hbm(history), in_hbm(weights), *after)


def turn_propagator(propagator, where, after):
    cols = propagator.shape[1]
    part = cols // 8
    blocks = in_hbm(propagator.reshape(8, 2, 8, part, cols))

    def kernel(at, *refs):
        ins, outs = refs[:4], refs[5:]
        for n in range(2):
            both = jnp.concatenate([ins[2 * n][0, 0, 0], ins[2 * n + 1][0, 0, 0]], axis=0)
            outs[2 * n][...], outs[2 * n + 1][...] = split(both.T)

    def spec(core, odd):
        return pl.BlockSpec(
            (1, 1, 1, part, cols), lambda q, at: (at[2 * q + odd], at[8] ^ core, at[9], 0, 0)
        )

    return pl.pallas_call(
        kernel,
        grid_spec=pltpu.PrefetchScalarGridSpec(
            num_scalar_prefetch=1,
            grid=(4,),
            in_specs=[spec(core, odd) for core in range(2) for odd in range(2)] + [UNREAD],
            out_specs=[pl.BlockSpec((cols, 2 * part), lambda q, at: (0, q))] * 4,
        ),
        out_shape=[jax.ShapeDtypeStruct((cols, 8 * part), BF16)] * 4,
        name="turn_propagator",
        compiler_params=pltpu.CompilerParams(vmem_limit_bytes=8 << 20),
    )(where, *[blocks] * 4, after)


def turn_explicit(explicit_one, explicit_two, where, after):
    size = explicit_one.shape[0]
    part = explicit_one.shape[1] // 8

    def kernel(at, first_ref, second_ref, _, *rest):
        turned = rest[2]
        for ref, out in ((first_ref, rest[0]), (second_ref, rest[1])):
            turned[...] = ref[...].T
            out[...] = turned[rows_from((at[0] & 1) * part, part), :]

    narrow = pl.BlockSpec((size, 2 * part), lambda i, at: (0, at[0] >> 1))
    return pl.pallas_call(
        kernel,
        grid_spec=pltpu.PrefetchScalarGridSpec(
            num_scalar_prefetch=1,
            grid=(1,),
            in_specs=[narrow, narrow, UNREAD],
            out_specs=[WHOLE] * 2,
            scratch_shapes=[pltpu.VMEM((2 * part, size), F32)],
        ),
        out_shape=[jax.ShapeDtypeStruct((part, size), F32)] * 2,
        name="turn_explicit",
        compiler_params=pltpu.CompilerParams(vmem_limit_bytes=4 << 20),
    )(where, in_hbm(explicit_one), in_hbm(explicit_two), after)


def turn_matrices(inverse_one, link, inverse_two, where, after):
    size = link.shape[0]
    half = size // 2

    def kernel(at, one_ref, link_ref, two_ref, *outs):
        outs[0][...], outs[1][...] = split(one_ref[...].T)
        outs[2][...], outs[3][...] = split(link_ref[...].T)
        far = two_ref[rows_from((at[0] ^ 1) * half, half), :]
        near = two_ref[rows_from(at[0] * half, half), :]
        outs[4][:, :half], outs[5][:, :half] = split(far.T)
        outs[4][:, half:], outs[5][:, half:] = split(near.T)

    outs = [((size, size), BF16)] * 6
    return call(kernel, outs, "turn_matrices", where, [inverse_one, link, inverse_two], [after])


def predict(explicit, parts, where, after):
    def kernel(at, *refs):
        pred = total(refs[:-2])
        refs[-2][...] = pred
        refs[-1][...] = cubic_power(pred)

    outs = [(explicit.shape, F32)] * 2
    return call(kernel, outs, "predict", where, [explicit, *parts], after)


def propagate(turned, blocks, where, span, begun=(), after=()):
    def kernel(at, high_ref, low_ref, *refs):
        blocks_in = jnp.concatenate([ref[...] for ref in refs[: len(blocks)]], axis=0)
        value = product((high_ref[:, span], low_ref[:, span]), split(blocks_in))
        for ref in refs[len(blocks) : -1]:
            value = value + ref[...]
        refs[-1][...] = value

    outs = [((turned[0].shape[0], blocks[0].shape[1]), F32)]
    return call(kernel, outs, "propagate", where, [*turned, *blocks, *begun], after)[0]


def finish_first(turned, blocks, where, span, begun):
    size, rows = begun.shape
    part = size // 8
    n = len(blocks)

    def kernel(at, high_ref, low_ref, *refs):
        outs, acc = refs[n + 1 : -1], refs[-1]
        blocks_in = jnp.concatenate([ref[...] for ref in refs[:n]], axis=0)
        acc[...] = refs[n][...] + product((high_ref[:, span], low_ref[:, span]), split(blocks_in))
        for near in range(2):
            for d in range(4):
                member = (at[0] ^ (1 - near)) * 4 + ((at[1] + d) & 3)
                outs[near * 4 + d][...] = acc[rows_from(member * part, part), :]

    outs = [((part, rows), F32)] * 8
    inputs = [*turned, *blocks, begun]
    return call(kernel, outs, "finish_first", where, inputs, (), [(size, rows)])


def finish_second(turned, blocks, where, span, begun, kept, after):
    cols, rows = begun.shape
    part = cols // 8
    n = len(blocks)

    def kernel(at, high_ref, low_ref, *refs):
        outs, acc, flipped = refs[n + 2 : -2], refs[-2], refs[-1]
        blocks_in = jnp.concatenate([ref[...] for ref in refs[:n]], axis=0)
        acc[...] = refs[n][...] + product((high_ref[:, span], low_ref[:, span]), split(blocks_in))
        mine = rows_from(at[1] * part, part)
        acc[mine, :] = acc[mine, :] + refs[n + 1][...]
        flipped[...] = acc[...].T
        for near in range(2):
            for d in range(4):
                member = near * 4 + ((at[0] + d) & 3)
                outs[near * 4 + d][...] = flipped[rows_from(member * part, part), :]

    outs = [((part, cols), F32)] * 8
    inputs = [*turned, *blocks, begun, kept]
    scratch = [(cols, rows), (rows, cols)]
    return call(kernel, outs, "finish_second", where, inputs, after, scratch)


def solve(pred_one, parts, matrices, explicit_two, near_parts, where):
    part, size = pred_one.shape
    n = len(parts)

    def kernel(at, pred_ref, explicit_ref, keep_ref, near_ref, *rest):
        ins, mats = rest[:n], rest[n : n + 6]
        kept_ref, moved_ref, far_out, near_out, turned = rest[n + 6 :]
        right = pred_ref[...] + step_size * total(ins)
        first = product(split(right), (mats[0][...], mats[1][...]))
        pred = explicit_ref[...] + (keep_ref[...] + near_ref[...])
        pred = pred + product(split(cubic_power(first)), (mats[2][...], mats[3][...]))
        both = jnp.concatenate([step_size * cubic_power(pred), pred], axis=0)
        solved = product(split(both), (mats[4][...], mats[5][...]))
        kept_ref[...] = solved[part:]
        moved_ref[...] = solved[:part]
        turned[...] = jnp.concatenate([first, first], axis=0).T
        for d in range(4):
            place = (at[1] + d) & 3
            far_out[d] = turned[rows_from(((at[0] ^ 1) * 4 + place) * part, part), :]
            near_out[d] = turned[rows_from((at[0] * 4 + place) * part, part), :]

    outs = [((part, size), F32)] * 2 + [((4, part, 2 * part), F32)] * 2
    inputs = [pred_one, explicit_two, *near_parts, *parts, *matrices]
    return call(kernel, outs, "solve", where, inputs, (), [(size, 2 * part)])


def add_near(blocks, where, after):
    def kernel(at, *refs):
        ins, far_ref, keep_ref = refs[:4], refs[4], refs[5]
        far_ref[...] = (ins[0][0] + ins[1][0]) + (ins[2][0] + ins[3][0])
        keep_ref[...] = (ins[0][1] + ins[1][1]) + (ins[2][1] + ins[3][1])

    return call(kernel, [(blocks[0].shape[1:], F32)] * 2, "add_near", where, blocks, after)


def pair_up(near, far, where, after):
    def kernel(at, near_ref, far_ref, *outs):
        for d in range(4):
            outs[d][0] = near_ref[d]
            outs[d][1] = far_ref[d]

    outs = [((2, *near.shape[1:]), F32)] * 4
    return call(kernel, outs, "pair_up", where, [near, far], after)


def place_rows(pairs, where):
    part, width = pairs[0].shape[1:]

    def kernel(at, *refs):
        ins, out_ref, sorted_ref = refs[:4], refs[4], refs[5]
        for d in range(4):
            for n in range(2):
                sorted_ref[(at[0] ^ n) * 4 + ((at[1] - d) & 3)] = ins[d][n]
        lower = lax.broadcasted_iota(jnp.int32, (part, width), 1) < part
        for b in range(4):
            out_ref[:, b * width : (b + 1) * width] = jnp.where(
                lower, sorted_ref[2 * b], sorted_ref[2 * b + 1]
            )

    outs = [((part, 4 * width), F32)]
    return call(kernel, outs, "place_rows", where, pairs, (), [(8, part, width)])[0]


def add_all(parts, where):
    def kernel(at, *refs):
        refs[-1][...] = total(refs[:-1])

    return call(kernel, [(parts[0].shape, F32)], "add_all", where, parts)[0]


def exchange(blocks):
    far = [move_hist(blocks[d], 1, d) for d in (2, 1, 3, 0)]
    return [blocks[4]] + far + [move_hist(blocks[4 + d], 0, d) for d in (2, 1, 3)]


def shards(
    history,
    memory_weight_first,
    memory_weight_second,
    link,
    propagator,
    inverse_one,
    inverse_two,
    explicit_first,
    explicit_second,
):
    h = lax.axis_index("hist")
    t = lax.axis_index("tcol")
    z, x = h >> 2, h & 3
    chip_z, chip_y, core = t >> 3, (t >> 1) & 3, t & 1
    part = explicit_first.shape[1] // 8

    def numbers(*values):
        return jnp.stack([v.astype(jnp.int32) for v in values])

    zx, xh = numbers(z, x), numbers(x, h)
    sources = [(chip_z ^ dz) * 4 + ((chip_y - dy) & 3) for dz, dy in CHIPS]
    early, late = slice(0, 4 * part), slice(4 * part, 8 * part)

    blocks = collect(history, memory_weight_first, zx, False)
    parts = exchange(blocks)
    near_blocks = collect(history, memory_weight_second, zx, True, [blocks[0]])
    explicit_one, explicit_two = turn_explicit(
        explicit_first, explicit_second, numbers(h), blocks[0]
    )
    near_parts = [near_blocks[0]] + [move_hist(near_blocks[d], 0, d) for d in (2, 1, 3)]
    pred_one, sigma = predict(explicit_one, parts, zx, [near_blocks[0]])

    def spread(value):
        own = [value] + [move_tcol(value, dz, dy) for dz, dy in CHIPS[1:]]
        return own, [other_core(block) for block in own]

    own, other = spread(sigma)
    turned = turn_propagator(propagator, numbers(*sources, core, h), sigma)
    matrices = turn_matrices(inverse_one, link, inverse_two, zx, turned[0])
    mine, theirs = turned[:2], turned[2:]
    begun = propagate(mine, own[:4], zx, early, (), [matrices[0]])
    begun = propagate(theirs, other[:4], zx, early, [begun])
    begun = propagate(mine, own[4:], zx, late, [begun])
    blocks = finish_first(theirs, other[4:], zx, late, begun)
    parts = exchange(blocks)

    far, keep = add_near(near_parts, zx, [blocks[0]])
    near = move_hist(far, 1, 0)

    kept, moved, far_rows, near_rows = solve(
        pred_one, parts, matrices, explicit_two, (keep, near), zx
    )
    own, other = spread(moved)
    pairs = pair_up(near_rows, move_hist(far_rows, 1, 0), zx, ())
    placed = place_rows([pairs[0]] + [move_hist(pairs[d], 0, d) for d in (1, 2, 3)], zx)
    begun = propagate(mine, own[:4], zx, early, (), [pairs[0]])
    begun = propagate(theirs, other[:4], zx, early, [begun])
    begun = propagate(mine, own[4:], zx, late, [begun])
    blocks = finish_second(theirs, other[4:], xh, late, begun, kept, ())
    slab_two = add_all(exchange(blocks), zx)
    return placed, slab_two


def solution(mesh):
    return jax.shard_map(
        shards,
        mesh=mesh,
        in_specs=(
            P("hist", "tcol"),
            P(None, "hist"),
            P(None, "hist"),
            P(),
            P(None, "tcol"),
            P(),
            P(),
            P(None, "tcol"),
            P(None, "tcol"),
        ),
        out_specs=(P("hist", "tcol"), P("hist", "tcol")),
        check_vma=False,
    )
```

```python
import jax
import jax.numpy as jnp
from jax import lax
from jax.experimental import pallas as pl
from jax.experimental.pallas import tpu as pltpu
from jax.sharding import PartitionSpec as P

strength = 0.2
step_size = 0.5
F32, BF16 = jnp.float32, jnp.bfloat16
WHOLE = pl.BlockSpec(memory_space=pltpu.VMEM)
SCALARS = pl.BlockSpec(memory_space=pltpu.SMEM)
CHUNK = 512
LANES = 128
UNREAD = pl.BlockSpec(memory_space=pl.ANY)

CHIPS = ((0, 0), (1, 2), (1, 1), (1, 3), (0, 2), (1, 0), (0, 1), (0, 3))


def move_hist(value, dz, dx):
    pairs = [(i, ((i >> 2) ^ dz) * 4 + ((i & 3) + dx) % 4) for i in range(8)]
    return lax.ppermute(value, "hist", pairs)


def move_tcol(value, dz, dy):
    pairs = [
        (i, ((i >> 3) ^ dz) * 8 + ((((i >> 1) & 3) + dy) % 4) * 2 + (i & 1)) for i in range(16)
    ]
    return lax.ppermute(value, "tcol", pairs)


def other_core(value):
    return lax.ppermute(value, "tcol", [(i, i ^ 1) for i in range(16)])


def cubic_power(value):
    return strength * value * value * value


def split(value):
    high = value.astype(BF16)
    return high, (value - high.astype(F32)).astype(BF16)


def product(left, right):
    def dot(a, b):
        return jnp.dot(a, b, preferred_element_type=F32)

    return dot(left[0], right[0]) + (dot(left[0], right[1]) + dot(left[1], right[0]))


def total(refs):
    value = refs[0][...]
    for ref in refs[1:]:
        value = value + ref[...]
    return value


def rows_from(start, count):
    return pl.ds(pl.multiple_of(start, count), count)


def call(kernel, outs, name, where, inputs, after=(), scratch=()):
    n = len(after)

    def body(at, *refs):
        kernel(at, *refs[: len(inputs)], *refs[len(inputs) + n :])

    return pl.pallas_call(
        body,
        in_specs=[SCALARS] + [WHOLE] * len(inputs) + [UNREAD] * n,
        out_shape=[jax.ShapeDtypeStruct(shape, dtype) for shape, dtype in outs],
        out_specs=[WHOLE] * len(outs),
        scratch_shapes=[pltpu.VMEM(shape, F32) for shape in scratch],
        name=name,
        compiler_params=pltpu.CompilerParams(vmem_limit_bytes=8 << 20),
    )(where, *inputs, *after)


def in_hbm(array):
    return pltpu.with_memory_space_constraint(array, pltpu.HBM)


def lanes_from(block):
    return pl.ds(pl.multiple_of(block * LANES, LANES), LANES)


def collect(history, weights, where, cut, after=()):
    depth, cols = history.shape
    rows = weights.shape[0]
    half = rows // 2
    n = len(after)

    def kernel(at, hist_ref, weight_ref, *rest):
        step = pl.program_id(0)
        acc = rest[-1]

        @pl.when(step == 0)
        def _():
            acc[...] = jnp.zeros_like(acc)

        acc[...] += product(split(weight_ref[...]), split(cubic_power(hist_ref[...])))

        if cut:

            @pl.when(step == pl.num_programs(0) - 1)
            def _():
                for near in range(2):
                    lines = rows_from((at[0] ^ (1 - near)) * half, half)
                    for d in range(4):
                        rest[n + d][near] = acc[lines, lanes_from((at[1] + d) & 3)]

    shapes = [(2, half, LANES)] * 4 if cut else [(rows, cols)]
    return pl.pallas_call(
        kernel,
        grid_spec=pltpu.PrefetchScalarGridSpec(
            num_scalar_prefetch=1,
            grid=(depth // CHUNK,),
            in_specs=[
                pl.BlockSpec((CHUNK, cols), lambda r, at: (r, 0)),
                pl.BlockSpec((rows, CHUNK), lambda r, at: (0, r)),
            ]
            + [UNREAD] * n,
            out_specs=[WHOLE] * len(shapes),
            scratch_shapes=[pltpu.VMEM((rows, cols), F32)] if cut else [],
        ),
        out_shape=[jax.ShapeDtypeStruct(shape, F32) for shape in shapes],
        name="collect",
        compiler_params=pltpu.CompilerParams(vmem_limit_bytes=14 << 20),
    )(where, in_hbm(history), in_hbm(weights), *after)


def cut_sums(sums, where, after):
    def kernel(at, sums_ref, *outs):
        for d in range(4):
            outs[d][...] = sums_ref[:, lanes_from((at[1] + d) & 3)]

    outs = [((sums.shape[0], LANES), F32)] * 4
    return call(kernel, outs, "cut_sums", where, [sums], after)


def split_propagator(propagator, where, after):
    cols = propagator.shape[1]
    blocks = in_hbm(propagator.reshape(16, 4, LANES, cols))

    def kernel(at, *refs):
        ins, outs = refs[:4], refs[5:]
        for core in range(2):
            for odd in range(2):
                lines = slice(odd * LANES, (odd + 1) * LANES)
                high, low = split(ins[2 * core + odd][0, 0])
                outs[2 * core][lines], outs[2 * core + 1][lines] = high, low

    def spec(core, odd):
        return pl.BlockSpec(
            (1, 1, LANES, cols), lambda q, at: (at[2 * q + odd] ^ core, at[8], 0, 0)
        )

    return pl.pallas_call(
        kernel,
        grid_spec=pltpu.PrefetchScalarGridSpec(
            num_scalar_prefetch=1,
            grid=(4,),
            in_specs=[spec(core, odd) for core in range(2) for odd in range(2)] + [UNREAD],
            out_specs=[pl.BlockSpec((2 * LANES, cols), lambda q, at: (q, 0))] * 4,
        ),
        out_shape=[jax.ShapeDtypeStruct((8 * LANES, cols), BF16)] * 4,
        name="split_propagator",
        compiler_params=pltpu.CompilerParams(vmem_limit_bytes=12 << 20),
    )(where, *[blocks] * 4, after)


def own_explicit(explicit_one, explicit_two, where, after):
    size = explicit_one.shape[0]

    def kernel(at, first_ref, second_ref, _, first_out, second_out):
        first_out[...] = first_ref[...]
        second_out[...] = second_ref[...]

    return pl.pallas_call(
        kernel,
        grid_spec=pltpu.PrefetchScalarGridSpec(
            num_scalar_prefetch=1,
            grid=(1,),
            in_specs=[
                pl.BlockSpec((size // 2, LANES), lambda i, at: (at[0], at[1])),
                pl.BlockSpec((size, LANES), lambda i, at: (0, at[1])),
                UNREAD,
            ],
            out_specs=[WHOLE] * 2,
        ),
        out_shape=[
            jax.ShapeDtypeStruct((size // 2, LANES), F32),
            jax.ShapeDtypeStruct((size, LANES), F32),
        ],
        name="own_explicit",
        compiler_params=pltpu.CompilerParams(vmem_limit_bytes=4 << 20),
    )(where, in_hbm(explicit_one), in_hbm(explicit_two), after)


def split_matrices(matrices, where, after):
    size = matrices[0].shape[0]
    half = size // 2

    def kernel(at, *refs):
        for n in range(2):
            refs[3 + 2 * n][...], refs[4 + 2 * n][...] = split(refs[n][...])
        refs[7][...], refs[8][...] = split(refs[2][rows_from(at[0] * half, half), :])

    outs = [((size, size), BF16)] * 4 + [((half, size), BF16)] * 2
    return call(kernel, outs, "split_matrices", where, matrices, after)


def predict(explicit, parts, where, after):
    def kernel(at, *refs):
        pred = total(refs[:-2])
        refs[-2][...] = pred
        refs[-1][...] = cubic_power(pred)

    outs = [(explicit.shape, F32)] * 2
    return call(kernel, outs, "predict", where, [explicit, *parts], after)


def times(split_rows, refs, span):
    blocks = jnp.concatenate([ref[...] for ref in refs], axis=1)
    return product(split(blocks), (split_rows[0][span, :], split_rows[1][span, :]))


def propagate(split_rows, blocks, where, span, begun=(), after=()):
    n = len(blocks)

    def kernel(at, high_ref, low_ref, *refs):
        value = times((high_ref, low_ref), refs[:n], span)
        for ref in refs[n:-1]:
            value = value + ref[...]
        refs[-1][...] = value

    outs = [((blocks[0].shape[0], split_rows[0].shape[1]), F32)]
    return call(kernel, outs, "propagate", where, [*split_rows, *blocks, *begun], after)[0]


def finish_first(split_rows, blocks, where, span, begun):
    n = len(blocks)

    def kernel(at, high_ref, low_ref, *refs):
        acc = refs[-1]
        acc[...] = refs[n][...] + times((high_ref, low_ref), refs[:n], span)
        for d in range(4):
            refs[n + 1 + d][...] = acc[:, lanes_from((at[1] + d) & 3)]

    rows, cols = begun.shape
    outs = [((rows, LANES), F32)] * 4
    inputs = [*split_rows, *blocks, begun]
    return call(kernel, outs, "finish_first", where, inputs, (), [(rows, cols)])


def finish_second(split_rows, blocks, where, span, begun, kept, pieces):
    n = len(blocks)
    rows, cols = begun.shape
    part = rows // 4

    def kernel(at, high_ref, low_ref, *refs):
        outs, acc = refs[n + 3 : -1], refs[-1]
        acc[...] = refs[n][...] + times((high_ref, low_ref), refs[:n], span)
        mine = lanes_from(at[1])
        acc[:, mine] = acc[:, mine] + refs[n + 1][...]
        for d in range(4):
            outs[d][:, :cols] = acc[rows_from(((at[1] + d) & 3) * part, part), :]
            outs[d][:, cols:] = refs[n + 2][d]

    outs = [((part, cols + LANES), F32)] * 4
    inputs = [*split_rows, *blocks, begun, kept, pieces]
    return call(kernel, outs, "finish_second", where, inputs, (), [(rows, cols)])


def right_side(pred, parts, where):
    def kernel(at, pred_ref, *refs):
        refs[-1][...] = pred_ref[...] + step_size * total(refs[:-1])

    return call(kernel, [(pred.shape, F32)], "right_side", where, [pred, *parts])[0]


def solve(right_own, right_other, matrices, explicit_two, near_own, near_other, where):
    half = right_own.shape[0]
    part = half // 4

    def kernel(at, own_ref, other_ref, explicit_ref, near_ref, far_ref, *rest):
        mats, (moved_ref, kept_ref, piece_ref, right, first) = rest[:6], rest[6:]
        right[rows_from(at[0] * half, half), :] = own_ref[...]
        right[rows_from((at[0] ^ 1) * half, half), :] = other_ref[...]
        first[...] = product((mats[0][...], mats[1][...]), split(right[...]))
        pred = explicit_ref[...] + (near_ref[...] + far_ref[...])
        pred = pred + product((mats[2][...], mats[3][...]), split(cubic_power(first[...])))
        both = jnp.concatenate([step_size * cubic_power(pred), pred], axis=1)
        solved = product((mats[4][...], mats[5][...]), split(both))
        moved_ref[...] = solved[:, :LANES]
        kept_ref[...] = solved[:, LANES:]
        for d in range(4):
            piece_ref[d] = first[rows_from((at[0] * 4 + ((at[1] + d) & 3)) * part, part), :]

    outs = [((half, LANES), F32)] * 2 + [((4, part, LANES), F32)]
    inputs = [right_own, right_other, explicit_two, near_own, near_other, *matrices]
    return call(kernel, outs, "solve", where, inputs, (), [(2 * half, LANES)] * 2)


def add_pairs(blocks, where, after):
    def kernel(at, *refs):
        ins, far_ref, keep_ref = refs[:4], refs[4], refs[5]
        far_ref[...] = (ins[0][0] + ins[1][0]) + (ins[2][0] + ins[3][0])
        keep_ref[...] = (ins[0][1] + ins[1][1]) + (ins[2][1] + ins[3][1])

    return call(kernel, [(blocks[0].shape[1:], F32)] * 2, "add_pairs", where, blocks, after)


def add_blocks(blocks, where, after):
    def kernel(at, *refs):
        refs[-1][...] = total(refs[:-1])

    return call(kernel, [(blocks[0].shape, F32)], "add_blocks", where, blocks, after)[0]


def last_rows(parts, where):
    part, width = parts[0].shape
    cols = width - LANES

    def kernel(at, *refs):
        first_ref, second_ref = refs[4], refs[5]
        second_ref[...] = total([ref.at[:, :cols] for ref in refs[:4]])
        for ref, d in zip(refs, (0, 2, 1, 3)):
            first_ref[:, lanes_from((at[1] - d) & 3)] = ref[:, cols:]

    return call(kernel, [((part, cols), F32)] * 2, "last_rows", where, parts)


def shards(
    history,
    memory_weight_first,
    memory_weight_second,
    link,
    propagator,
    inverse_one,
    inverse_two,
    explicit_first,
    explicit_second,
):
    h = lax.axis_index("hist")
    t = lax.axis_index("tcol")
    z, x = h >> 2, h & 3
    chip_z, chip_y, core = t >> 3, (t >> 1) & 3, t & 1

    def numbers(*values):
        return jnp.stack([v.astype(jnp.int32) for v in values])

    zx = numbers(z, x)
    sources = [(chip_z ^ dz) * 8 + ((chip_y - dy) & 3) * 2 + core for dz, dy in CHIPS]
    early = 4
    span_early, span_late = slice(0, early * LANES), slice(early * LANES, 8 * LANES)

    def over_x(blocks):
        return [blocks[0]] + [move_hist(blocks[d], 0, d) for d in (2, 1, 3)]

    def spread(value):
        own = [value] + [move_tcol(value, dz, dy) for dz, dy in CHIPS[1:]]
        return own, [other_core(block) for block in own]

    blocks = collect(history, memory_weight_first, zx, True)
    pairs = over_x(blocks)
    sums = collect(history, memory_weight_second, zx, False, [blocks[0]])[0]
    explicit_one, explicit_two = own_explicit(explicit_first, explicit_second, zx, sums)
    far, keep = add_pairs(pairs, zx, [sums])
    other_z = move_hist(far, 1, 0)
    near_blocks = over_x(cut_sums(sums, zx, [far]))
    pred_one, sigma = predict(explicit_one, [keep, other_z], zx, [near_blocks[0]])

    own, other = spread(sigma)
    rows = split_propagator(propagator, numbers(*sources, x), sigma)
    mine, theirs = rows[:2], rows[2:]
    begun = propagate(mine, own[:early], zx, span_early)
    begun = propagate(theirs, other[:early], zx, span_early, [begun])
    begun = propagate(mine, own[early:], zx, span_late, [begun])
    blocks = finish_first(theirs, other[early:], zx, span_late, begun)
    matrices = split_matrices([inverse_one, link, inverse_two], zx, [blocks[0]])
    parts = over_x(blocks)

    near = add_blocks(near_blocks, zx, [blocks[0]])
    near_other = move_hist(near, 1, 0)

    right = right_side(pred_one, parts, zx)
    moved, kept, pieces = solve(
        right, move_hist(right, 1, 0), matrices, explicit_two, near, near_other, zx
    )
    own, other = spread(moved)
    begun = propagate(mine, own[:early], zx, span_early)
    begun = propagate(theirs, other[:early], zx, span_early, [begun])
    begun = propagate(mine, own[early:], zx, span_late, [begun])
    blocks = finish_second(theirs, other[early:], zx, span_late, begun, kept, pieces)
    return tuple(last_rows(over_x(blocks), zx))


def solution(mesh):
    return jax.shard_map(
        shards,
        mesh=mesh,
        in_specs=(
            P("hist", "tcol"),
            P(None, "hist"),
            P(None, "hist"),
            P(),
            P(None, "tcol"),
            P(),
            P(),
            P(None, "tcol"),
            P(None, "tcol"),
        ),
        out_specs=(P("hist", "tcol"), P("hist", "tcol")),
        check_vma=False,
    )
```

```python
import jax
import jax.numpy as jnp
from jax import lax
from jax.experimental import pallas as pl
from jax.experimental.pallas import tpu as pltpu
from jax.sharding import PartitionSpec as P


strength = 0.2
step_size = 0.5
F32, BF16 = jnp.float32, jnp.bfloat16
WHOLE = pl.BlockSpec(memory_space=pltpu.VMEM)
SCALARS = pl.BlockSpec(memory_space=pltpu.SMEM)
CHUNKS = (256, 256, 512, 512, 512)
LANES = 128
UNREAD = pl.BlockSpec(memory_space=pl.ANY)

CHIPS = ((0, 0), (0, 1), (1, 1), (1, -1), (0, -1), (1, 0), (0, 2), (1, 2))


def move_hist(value, dz, dx):
    pairs = [(i, ((i >> 2) ^ dz) * 4 + ((i & 3) + dx) % 4) for i in range(8)]
    return lax.ppermute(value, "hist", pairs)


def move_tcol(value, dz, dy):
    def target(i):
        y = ((i >> 1) + (-dy if i & 1 else dy)) % 4
        return ((i >> 3) ^ dz) * 8 + y * 2 + (i & 1)

    return lax.ppermute(value, "tcol", [(i, target(i)) for i in range(16)])


def other_core(value):
    return lax.ppermute(value, "tcol", [(i, i ^ 1) for i in range(16)])


def cubic_power(value):
    return strength * value * value * value


def split(value):
    high = value.astype(BF16)
    return high, (value - high.astype(F32)).astype(BF16)


def product(left, right):
    def dot(a, b):
        return jnp.dot(a, b, preferred_element_type=F32)

    return dot(left[0], right[0]) + (dot(left[0], right[1]) + dot(left[1], right[0]))


def narrow_product(left, right):
    n = right[0].shape[1]
    wide = jnp.dot(left[0], jnp.concatenate(right, axis=1), preferred_element_type=F32)
    low = jnp.dot(left[1], right[0], preferred_element_type=F32)
    return wide[:, :n] + (wide[:, n:] + low)


def total(refs):
    value = refs[0][...]
    for ref in refs[1:]:
        value = value + ref[...]
    return value


def rows_from(start, count):
    return pl.ds(pl.multiple_of(start, count), count)


def call(kernel, outs, where, inputs, after=(), scratch=()):
    n = len(after)

    def body(at, *refs):
        kernel(at, *refs[: len(inputs)], *refs[len(inputs) + n :])

    return pl.pallas_call(
        body,
        in_specs=[SCALARS] + [WHOLE] * len(inputs) + [UNREAD] * n,
        out_shape=[jax.ShapeDtypeStruct(shape, dtype) for shape, dtype in outs],
        out_specs=[WHOLE] * len(outs),
        scratch_shapes=[pltpu.VMEM(shape, F32) for shape in scratch],
        compiler_params=pltpu.CompilerParams(vmem_limit_bytes=8 << 20),
    )(where, *inputs, *after)


def in_hbm(array):
    return pltpu.with_memory_space_constraint(array, pltpu.HBM)


def lanes_from(block):
    return pl.ds(pl.multiple_of(block * LANES, LANES), LANES)


def collect(history, weights, where, cut, after=()):
    depth, cols = history.shape
    rows = weights.shape[0]
    half = rows // 2
    n = len(after)
    ends = [depth * sum(CHUNKS[: r + 1]) // sum(CHUNKS) for r in range(len(CHUNKS))]
    steps = len(ends)
    shapes = [(2, half, LANES)] * 4 if cut else [(rows, cols)]

    def kernel(at, hist_ref, weight_ref, *rest):
        outs = rest[n : n + len(shapes)]
        hist, weight, arrived = rest[n + len(shapes) : n + len(shapes) + 3]
        acc = rest[-1] if cut else outs[0]
        copies = []
        for r in range(steps):
            lines = slice(ends[r - 1] if r else 0, ends[r])
            pair = (
                pltpu.make_async_copy(hist_ref.at[lines, :], hist.at[lines, :], arrived.at[r, 0]),
                pltpu.make_async_copy(
                    weight_ref.at[:, lines], weight.at[:, lines], arrived.at[r, 1]
                ),
            )
            for copy in pair:
                copy.start()
            copies.append((lines, pair))
        for r, (lines, pair) in enumerate(copies):
            for copy in pair:
                copy.wait()
            value = product(split(weight[:, lines]), split(cubic_power(hist[lines, :])))
            acc[...] = value if r == 0 else acc[...] + value
        if cut:
            for near in range(2):
                lines = rows_from((at[0] ^ (1 - near)) * half, half)
                for d in range(4):
                    outs[d][near] = acc[lines, lanes_from((at[1] + d) & 3)]

    scratch = [
        pltpu.VMEM((depth, cols), F32),
        pltpu.VMEM((rows, depth), F32),
        pltpu.SemaphoreType.DMA((steps, 2)),
    ]
    return pl.pallas_call(
        kernel,
        in_specs=[SCALARS, UNREAD, UNREAD] + [UNREAD] * n,
        out_specs=[WHOLE] * len(shapes),
        scratch_shapes=scratch + ([pltpu.VMEM((rows, cols), F32)] if cut else []),
        out_shape=[jax.ShapeDtypeStruct(shape, F32) for shape in shapes],
        name="collect",
        compiler_params=pltpu.CompilerParams(vmem_limit_bytes=20 << 20),
    )(where, in_hbm(history), in_hbm(weights), *after)


def cut_sums(sums, where, after):
    def kernel(at, sums_ref, *outs):
        for d in range(4):
            outs[d][...] = sums_ref[:, lanes_from((at[1] + d) & 3)]

    outs = [((sums.shape[0], LANES), F32)] * 4
    return call(kernel, outs, where, [sums], after)


def split_propagator(propagator, where, after):
    cols = propagator.shape[1]
    blocks = in_hbm(propagator.reshape(16, 4, LANES, cols))

    def kernel(at, blocks_ref, _, *refs):
        outs, held, arrived = refs[:4], refs[4], refs[5]
        copies = [
            pltpu.make_async_copy(blocks_ref.at[at[k], at[16]], held.at[k], arrived.at[k])
            for k in range(16)
        ]
        for copy in copies:
            copy.start()
        for k, copy in enumerate(copies):
            copy.wait()
            lines = slice((k & 7) * LANES, ((k & 7) + 1) * LANES)
            high, low = split(held[k])
            outs[2 * (k >> 3)][lines, :], outs[2 * (k >> 3) + 1][lines, :] = high, low

    return pl.pallas_call(
        kernel,
        in_specs=[SCALARS, UNREAD, UNREAD],
        out_specs=[WHOLE] * 4,
        scratch_shapes=[pltpu.VMEM((16, LANES, cols), F32), pltpu.SemaphoreType.DMA((16,))],
        out_shape=[jax.ShapeDtypeStruct((8 * LANES, cols), BF16)] * 4,
        name="split_propagator",
        compiler_params=pltpu.CompilerParams(vmem_limit_bytes=12 << 20),
    )(where, blocks, after)


def own_explicit(explicit_one, explicit_two, where, after):
    size = explicit_one.shape[0]

    def kernel(at, first_ref, second_ref, _, first_out, second_out):
        first_out[...] = first_ref[...]
        second_out[...] = second_ref[...]

    return pl.pallas_call(
        kernel,
        grid_spec=pltpu.PrefetchScalarGridSpec(
            num_scalar_prefetch=1,
            grid=(1,),
            in_specs=[
                pl.BlockSpec((size // 2, LANES), lambda i, at: (at[0], at[1])),
                pl.BlockSpec((size, LANES), lambda i, at: (0, at[1])),
                UNREAD,
            ],
            out_specs=[WHOLE] * 2,
        ),
        out_shape=[
            jax.ShapeDtypeStruct((size // 2, LANES), F32),
            jax.ShapeDtypeStruct((size, LANES), F32),
        ],
        name="own_explicit",
        compiler_params=pltpu.CompilerParams(vmem_limit_bytes=4 << 20),
    )(where, in_hbm(explicit_one), in_hbm(explicit_two), after)


def split_matrices(matrices, where, after):
    size = matrices[0].shape[0]
    half = size // 2

    def kernel(at, *refs):
        for n in range(2):
            refs[3 + 2 * n][...], refs[4 + 2 * n][...] = split(refs[n][...])
        refs[7][...], refs[8][...] = split(refs[2][rows_from(at[0] * half, half), :])

    outs = [((size, size), BF16)] * 4 + [((half, size), BF16)] * 2
    return call(kernel, outs, where, matrices, after)


def predict(explicit, parts, where, after):
    def kernel(at, *refs):
        pred = total(refs[:-2])
        refs[-2][...] = pred
        refs[-1][...] = cubic_power(pred)

    outs = [(explicit.shape, F32)] * 2
    return call(kernel, outs, where, [explicit, *parts], after)


def side_by_side(refs):
    return jnp.concatenate([ref[...] for ref in refs], axis=1)


def times(split_rows, blocks, span):
    return product(split(blocks), (split_rows[0][span, :], split_rows[1][span, :]))


def propagate(split_rows, blocks, where, span, begun=(), stacked=False):
    n = len(blocks)

    def kernel(at, high_ref, low_ref, *refs):
        joined = side_by_side(refs[:n])
        value = times((high_ref, low_ref), joined, span)
        for ref in refs[n : n + len(begun)]:
            value = value + ref[...]
        refs[n + len(begun)][...] = value
        if stacked:
            refs[-1][...] = joined

    rows = blocks[0].shape[0]
    outs = [((rows, split_rows[0].shape[1]), F32)]
    if stacked:
        outs.append(((rows, span.stop - span.start), F32))
    return call(kernel, outs, where, [*split_rows, *blocks, *begun])


def finish_first(split_rows, blocks, where, span, begun):
    n = len(blocks)

    def kernel(at, high_ref, low_ref, *refs):
        acc = refs[-1]
        acc[...] = refs[n][...] + times((high_ref, low_ref), side_by_side(refs[:n]), span)
        for d in range(4):
            refs[n + 1 + d][...] = acc[:, lanes_from((at[1] + d) & 3)]

    rows, cols = begun.shape
    outs = [((rows, LANES), F32)] * 4
    inputs = [*split_rows, *blocks, begun]
    return call(kernel, outs, where, inputs, (), [(rows, cols)])


def finish_second(split_rows, blocks, where, span, begun, kept):
    n = len(blocks)
    rows, cols = begun.shape
    part = rows // 4

    def kernel(at, high_ref, low_ref, *refs):
        outs, acc = refs[n + 2 : -1], refs[-1]
        acc[...] = refs[n][...] + times((high_ref, low_ref), side_by_side(refs[:n]), span)
        mine = lanes_from(at[1])
        acc[:, mine] = acc[:, mine] + refs[n + 1][...]
        for d in range(4):
            outs[d][...] = acc[rows_from(((at[1] + d) & 3) * part, part), :]

    outs = [((part, cols), F32)] * 4
    inputs = [*split_rows, *blocks, begun, kept]
    return call(kernel, outs, where, inputs, (), [(rows, cols)])


def right_side(pred, parts, where):
    def kernel(at, pred_ref, *refs):
        refs[-1][...] = pred_ref[...] + step_size * total(refs[:-1])

    return call(kernel, [(pred.shape, F32)], where, [pred, *parts])[0]


def solve(right_own, right_other, matrices, explicit_two, near_own, near_other, where):
    half = right_own.shape[0]
    part = half // 4

    def kernel(at, own_ref, other_ref, explicit_ref, near_ref, far_ref, *rest):
        mats, (moved_ref, kept_ref), pieces = rest[:6], rest[6:8], rest[8:12]
        right, first = rest[12:]
        right[rows_from(at[0] * half, half), :] = own_ref[...]
        right[rows_from((at[0] ^ 1) * half, half), :] = other_ref[...]
        first[...] = narrow_product((mats[0][...], mats[1][...]), split(right[...]))
        pred = explicit_ref[...] + (near_ref[...] + far_ref[...])
        pred = pred + narrow_product((mats[2][...], mats[3][...]), split(cubic_power(first[...])))
        both = jnp.concatenate([step_size * cubic_power(pred), pred], axis=1)
        solved = product((mats[4][...], mats[5][...]), split(both))
        moved_ref[...] = solved[:, :LANES]
        kept_ref[...] = solved[:, LANES:]
        for d in range(4):
            pieces[d][...] = first[rows_from((at[0] * 4 + ((at[1] + d) & 3)) * part, part), :]

    outs = [((half, LANES), F32)] * 2 + [((part, LANES), F32)] * 4
    inputs = [right_own, right_other, explicit_two, near_own, near_other, *matrices]
    return call(kernel, outs, where, inputs, (), [(2 * half, LANES)] * 2)


def add_pairs(blocks, where, after):
    def kernel(at, *refs):
        ins, far_ref, keep_ref = refs[:4], refs[4], refs[5]
        far_ref[...] = (ins[0][0] + ins[1][0]) + (ins[2][0] + ins[3][0])
        keep_ref[...] = (ins[0][1] + ins[1][1]) + (ins[2][1] + ins[3][1])

    return call(kernel, [(blocks[0].shape[1:], F32)] * 2, where, blocks, after)


def add_blocks(blocks, where, after):
    def kernel(at, *refs):
        refs[-1][...] = total(refs[:-1])

    return call(kernel, [(blocks[0].shape, F32)], where, blocks, after)[0]


def last_rows(pieces, parts, where):
    part, cols = parts[0].shape

    def kernel(at, *refs):
        first_ref, second_ref = refs[8], refs[9]
        second_ref[...] = total(refs[4:8])
        for ref, d in zip(refs[:4], (0, 2, 1, 3)):
            first_ref[:, lanes_from((at[1] - d) & 3)] = ref[...]

    outs = [((part, cols), F32)] * 2
    return call(kernel, outs, where, [*pieces, *parts])


def shards(
    history,
    memory_weight_first,
    memory_weight_second,
    link,
    propagator,
    inverse_one,
    inverse_two,
    explicit_first,
    explicit_second,
):
    h = lax.axis_index("hist")
    t = lax.axis_index("tcol")
    z, x = h >> 2, h & 3
    chip_z, chip_y, core = t >> 3, (t >> 1) & 3, t & 1

    def numbers(*values):
        return jnp.stack([v.astype(jnp.int32) for v in values])

    zx = numbers(z, x)
    sources = [
        (chip_z ^ dz) * 8 + ((chip_y - dy * (1 - 2 * c)) & 3) * 2 + c
        for c in (core, 1 - core)
        for dz, dy in CHIPS
    ]
    early = 6
    span_early, span_late = slice(0, early * LANES), slice(early * LANES, 8 * LANES)

    def over_x(blocks):
        return [blocks[0]] + [move_hist(blocks[d], 0, d) for d in (2, 1, 3)]

    def gathered(value):
        mine, theirs = rows[:2], rows[2:]
        own = [value] + [move_tcol(value, dz, dy) for dz, dy in CHIPS[1:6]]
        own += [move_tcol(own[1], 0, 1), move_tcol(own[2], 0, 1)]
        begun, stack = propagate(mine, own[:early], zx, span_early, (), True)
        first = other_core(stack)
        begun, stack = propagate(mine, own[early:], zx, span_late, [begun], True)
        last = other_core(stack)
        return propagate(theirs, [first], zx, span_early, [begun])[0], last

    blocks = collect(history, memory_weight_first, zx, True)
    pairs = over_x(blocks)
    sums = collect(history, memory_weight_second, zx, False, [blocks[0]])[0]
    explicit_one, explicit_two = own_explicit(explicit_first, explicit_second, zx, sums)
    far, keep = add_pairs(pairs, zx, [sums])
    other_z = move_hist(far, 1, 0)
    near_blocks = cut_sums(sums, zx, [far])
    near_blocks = over_x(near_blocks)
    pred_one, sigma = predict(explicit_one, [keep, other_z], zx, [near_blocks[0]])

    rows = split_propagator(propagator, numbers(*sources, x), sums)
    begun, block = gathered(sigma)
    blocks = finish_first(rows[2:], [block], zx, span_late, begun)
    matrices = split_matrices([inverse_one, link, inverse_two], zx, [blocks[0]])
    parts = over_x(blocks)

    near = add_blocks(near_blocks, zx, [blocks[0]])
    near_other = move_hist(near, 1, 0)

    right = right_side(pred_one, parts, zx)
    moved, kept, *pieces = solve(
        right, move_hist(right, 1, 0), matrices, explicit_two, near, near_other, zx
    )
    begun, block = gathered(moved)
    pieces = over_x(pieces)
    blocks = finish_second(rows[2:], [block], zx, span_late, begun, kept)
    return tuple(last_rows(pieces, over_x(blocks), zx))


def solution(mesh):
    return jax.shard_map(
        shards,
        mesh=mesh,
        in_specs=(
            P("hist", "tcol"),
            P(None, "hist"),
            P(None, "hist"),
            P(),
            P(None, "tcol"),
            P(),
            P(),
            P(None, "tcol"),
            P(None, "tcol"),
        ),
        out_specs=(P("hist", "tcol"), P("hist", "tcol")),
        check_vma=False,
    )
```

```python
import jax
import jax.numpy as jnp
from jax import lax
from jax.experimental import pallas as pl
from jax.experimental.pallas import tpu as pltpu
from jax.sharding import PartitionSpec as P


strength = 0.2
step_size = 0.5
F32, BF16 = jnp.float32, jnp.bfloat16
WHOLE = pl.BlockSpec(memory_space=pltpu.VMEM)
SCALARS = pl.BlockSpec(memory_space=pltpu.SMEM)
CHUNKS = (256, 256, 512, 512, 512)
LANES = 128
UNREAD = pl.BlockSpec(memory_space=pl.ANY)

CHIPS = ((0, 0), (0, 1), (1, 1), (1, -1), (0, -1), (1, 0), (0, 2), (1, 2))


def move_hist(value, dz, dx):
    pairs = [(i, ((i >> 2) ^ dz) * 4 + ((i & 3) + dx) % 4) for i in range(8)]
    return lax.ppermute(value, "hist", pairs)


def move_tcol(value, dz, dy):
    def target(i):
        y = ((i >> 1) + (-dy if i & 1 else dy)) % 4
        return ((i >> 3) ^ dz) * 8 + y * 2 + (i & 1)

    return lax.ppermute(value, "tcol", [(i, target(i)) for i in range(16)])


def other_core(value):
    return lax.ppermute(value, "tcol", [(i, i ^ 1) for i in range(16)])


def cubic_power(value):
    return strength * value * value * value


def split(value):
    high = value.astype(BF16)
    return high, (value - high.astype(F32)).astype(BF16)


def product(left, right):
    def dot(a, b):
        return jnp.dot(a, b, preferred_element_type=F32)

    return dot(left[0], right[0]) + (dot(left[0], right[1]) + dot(left[1], right[0]))


def narrow_product(left, right):
    n = right[0].shape[1]
    wide = jnp.dot(left[0], jnp.concatenate(right, axis=1), preferred_element_type=F32)
    low = jnp.dot(left[1], right[0], preferred_element_type=F32)
    return wide[:, :n] + (wide[:, n:] + low)


def total(refs):
    value = refs[0][...]
    for ref in refs[1:]:
        value = value + ref[...]
    return value


def rows_from(start, count):
    return pl.ds(pl.multiple_of(start, count), count)


def call(kernel, outs, where, inputs, after=(), scratch=()):
    n = len(after)

    def body(at, *refs):
        kernel(at, *refs[: len(inputs)], *refs[len(inputs) + n :])

    return pl.pallas_call(
        body,
        in_specs=[SCALARS] + [WHOLE] * len(inputs) + [UNREAD] * n,
        out_shape=[jax.ShapeDtypeStruct(shape, dtype) for shape, dtype in outs],
        out_specs=[WHOLE] * len(outs),
        scratch_shapes=[pltpu.VMEM(shape, F32) for shape in scratch],
        compiler_params=pltpu.CompilerParams(vmem_limit_bytes=8 << 20),
    )(where, *inputs, *after)


def in_hbm(array):
    return pltpu.with_memory_space_constraint(array, pltpu.HBM)


def lanes_from(block):
    return pl.ds(pl.multiple_of(block * LANES, LANES), LANES)


def collect(history, weights, where, cut, after=()):
    depth, cols = history.shape
    rows = weights.shape[0]
    half = rows // 2
    n = len(after)
    ends = [depth * sum(CHUNKS[: r + 1]) // sum(CHUNKS) for r in range(len(CHUNKS))]
    steps = len(ends)
    shapes = [(2, half, LANES)] * 4 if cut else [(rows, cols)]

    def kernel(at, hist_ref, weight_ref, *rest):
        outs = rest[n : n + len(shapes)]
        hist, weight, arrived = rest[n + len(shapes) : n + len(shapes) + 3]
        acc = rest[-1] if cut else outs[0]
        copies = []
        for r in range(steps):
            lines = slice(ends[r - 1] if r else 0, ends[r])
            pair = (
                pltpu.make_async_copy(hist_ref.at[lines, :], hist.at[lines, :], arrived.at[r, 0]),
                pltpu.make_async_copy(
                    weight_ref.at[:, lines], weight.at[:, lines], arrived.at[r, 1]
                ),
            )
            for copy in pair:
                copy.start()
            copies.append((lines, pair))
        for r, (lines, pair) in enumerate(copies):
            for copy in pair:
                copy.wait()
            value = product(split(weight[:, lines]), split(cubic_power(hist[lines, :])))
            acc[...] = value if r == 0 else acc[...] + value
        if cut:
            for near in range(2):
                lines = rows_from((at[0] ^ (1 - near)) * half, half)
                for d in range(4):
                    outs[d][near] = acc[lines, lanes_from((at[1] + d) & 3)]

    scratch = [
        pltpu.VMEM((depth, cols), F32),
        pltpu.VMEM((rows, depth), F32),
        pltpu.SemaphoreType.DMA((steps, 2)),
    ]
    return pl.pallas_call(
        kernel,
        in_specs=[SCALARS, UNREAD, UNREAD] + [UNREAD] * n,
        out_specs=[WHOLE] * len(shapes),
        scratch_shapes=scratch + ([pltpu.VMEM((rows, cols), F32)] if cut else []),
        out_shape=[jax.ShapeDtypeStruct(shape, F32) for shape in shapes],
        name="collect",
        compiler_params=pltpu.CompilerParams(vmem_limit_bytes=20 << 20),
    )(where, in_hbm(history), in_hbm(weights), *after)


def cut_sums(sums, where, after):
    def kernel(at, sums_ref, *outs):
        for d in range(4):
            outs[d][...] = sums_ref[:, lanes_from((at[1] + d) & 3)]

    outs = [((sums.shape[0], LANES), F32)] * 4
    return call(kernel, outs, where, [sums], after)


def split_propagator(propagator, where, after):
    cols = propagator.shape[1]
    blocks = in_hbm(propagator.reshape(16, 4, LANES, cols))

    def kernel(at, blocks_ref, _, *refs):
        outs, held, arrived = refs[:4], refs[4], refs[5]
        copies = [
            pltpu.make_async_copy(blocks_ref.at[at[k], at[16]], held.at[k], arrived.at[k])
            for k in range(16)
        ]
        for copy in copies:
            copy.start()
        for k, copy in enumerate(copies):
            copy.wait()
            lines = slice((k & 7) * LANES, ((k & 7) + 1) * LANES)
            high, low = split(held[k])
            outs[2 * (k >> 3)][lines, :], outs[2 * (k >> 3) + 1][lines, :] = high, low

    return pl.pallas_call(
        kernel,
        in_specs=[SCALARS, UNREAD, UNREAD],
        out_specs=[WHOLE] * 4,
        scratch_shapes=[pltpu.VMEM((16, LANES, cols), F32), pltpu.SemaphoreType.DMA((16,))],
        out_shape=[jax.ShapeDtypeStruct((8 * LANES, cols), BF16)] * 4,
        name="split_propagator",
        compiler_params=pltpu.CompilerParams(vmem_limit_bytes=12 << 20),
    )(where, blocks, after)


def split_matrices(matrices, where, after):
    size = matrices[0].shape[0]
    half = size // 2

    def kernel(at, *refs):
        for n in range(2):
            refs[3 + 2 * n][...], refs[4 + 2 * n][...] = split(refs[n][...])
        refs[7][...], refs[8][...] = split(refs[2][rows_from(at[0] * half, half), :])

    outs = [((size, size), BF16)] * 4 + [((half, size), BF16)] * 2
    return call(kernel, outs, where, matrices, after)


def predict(explicit, parts, where, after):
    half = explicit.shape[0] // 2

    def kernel(at, explicit_ref, *refs):
        pred = explicit_ref[rows_from(at[0] * half, half), lanes_from(at[1])] + total(refs[:-2])
        refs[-2][...] = pred
        refs[-1][...] = cubic_power(pred)

    outs = [((half, LANES), F32)] * 2
    return call(kernel, outs, where, [explicit, *parts], after)


def side_by_side(refs):
    return jnp.concatenate([ref[...] for ref in refs], axis=1)


def times(split_rows, blocks, span):
    return product(split(blocks), (split_rows[0][span, :], split_rows[1][span, :]))


def propagate(split_rows, blocks, where, span, begun=(), stacked=False):
    n = len(blocks)

    def kernel(at, high_ref, low_ref, *refs):
        joined = side_by_side(refs[:n])
        value = times((high_ref, low_ref), joined, span)
        for ref in refs[n : n + len(begun)]:
            value = value + ref[...]
        refs[n + len(begun)][...] = value
        if stacked:
            refs[-1][...] = joined

    rows = blocks[0].shape[0]
    outs = [((rows, split_rows[0].shape[1]), F32)]
    if stacked:
        outs.append(((rows, span.stop - span.start), F32))
    return call(kernel, outs, where, [*split_rows, *blocks, *begun])


def finish_first(split_rows, blocks, where, span, begun):
    n = len(blocks)

    def kernel(at, high_ref, low_ref, *refs):
        acc = refs[-1]
        acc[...] = refs[n][...] + times((high_ref, low_ref), side_by_side(refs[:n]), span)
        for d in range(4):
            refs[n + 1 + d][...] = acc[:, lanes_from((at[1] + d) & 3)]

    rows, cols = begun.shape
    outs = [((rows, LANES), F32)] * 4
    inputs = [*split_rows, *blocks, begun]
    return call(kernel, outs, where, inputs, (), [(rows, cols)])


def finish_second(split_rows, blocks, where, span, begun, kept):
    n = len(blocks)
    rows, cols = begun.shape
    part = rows // 4

    def kernel(at, high_ref, low_ref, *refs):
        outs, acc = refs[n + 2 : -1], refs[-1]
        acc[...] = refs[n][...] + times((high_ref, low_ref), side_by_side(refs[:n]), span)
        mine = lanes_from(at[1])
        acc[:, mine] = acc[:, mine] + refs[n + 1][...]
        for d in range(4):
            outs[d][...] = acc[rows_from(((at[1] + d) & 3) * part, part), :]

    outs = [((part, cols), F32)] * 4
    inputs = [*split_rows, *blocks, begun, kept]
    return call(kernel, outs, where, inputs, (), [(rows, cols)])


def right_side(pred, parts, where):
    def kernel(at, pred_ref, *refs):
        refs[-1][...] = pred_ref[...] + step_size * total(refs[:-1])

    return call(kernel, [(pred.shape, F32)], where, [pred, *parts])[0]


def solve(right_own, right_other, matrices, explicit_two, near_own, near_other, where):
    half = right_own.shape[0]
    part = half // 4

    def kernel(at, own_ref, other_ref, explicit_ref, near_ref, far_ref, *rest):
        mats, (moved_ref, kept_ref), pieces = rest[:6], rest[6:8], rest[8:12]
        right, first = rest[12:]
        right[rows_from(at[0] * half, half), :] = own_ref[...]
        right[rows_from((at[0] ^ 1) * half, half), :] = other_ref[...]
        first[...] = narrow_product((mats[0][...], mats[1][...]), split(right[...]))
        pred = explicit_ref[:, lanes_from(at[1])] + (near_ref[...] + far_ref[...])
        pred = pred + narrow_product((mats[2][...], mats[3][...]), split(cubic_power(first[...])))
        both = jnp.concatenate([step_size * cubic_power(pred), pred], axis=1)
        solved = product((mats[4][...], mats[5][...]), split(both))
        moved_ref[...] = solved[:, :LANES]
        kept_ref[...] = solved[:, LANES:]
        for d in range(4):
            pieces[d][...] = first[rows_from((at[0] * 4 + ((at[1] + d) & 3)) * part, part), :]

    outs = [((half, LANES), F32)] * 2 + [((part, LANES), F32)] * 4
    inputs = [right_own, right_other, explicit_two, near_own, near_other, *matrices]
    return call(kernel, outs, where, inputs, (), [(2 * half, LANES)] * 2)


def add_pairs(blocks, where, after):
    def kernel(at, *refs):
        ins, far_ref, keep_ref = refs[:4], refs[4], refs[5]
        far_ref[...] = (ins[0][0] + ins[1][0]) + (ins[2][0] + ins[3][0])
        keep_ref[...] = (ins[0][1] + ins[1][1]) + (ins[2][1] + ins[3][1])

    return call(kernel, [(blocks[0].shape[1:], F32)] * 2, where, blocks, after)


def add_blocks(blocks, where, after):
    def kernel(at, *refs):
        refs[-1][...] = total(refs[:-1])

    return call(kernel, [(blocks[0].shape, F32)], where, blocks, after)[0]


def last_rows(pieces, parts, where):
    part, cols = parts[0].shape

    def kernel(at, *refs):
        first_ref, second_ref = refs[8], refs[9]
        second_ref[...] = total(refs[4:8])
        for ref, d in zip(refs[:4], (0, 2, 1, 3)):
            first_ref[:, lanes_from((at[1] - d) & 3)] = ref[...]

    outs = [((part, cols), F32)] * 2
    return call(kernel, outs, where, [*pieces, *parts])


def shards(
    history,
    memory_weight_first,
    memory_weight_second,
    link,
    propagator,
    inverse_one,
    inverse_two,
    explicit_first,
    explicit_second,
):
    h = lax.axis_index("hist")
    t = lax.axis_index("tcol")
    z, x = h >> 2, h & 3
    chip_z, chip_y, core = t >> 3, (t >> 1) & 3, t & 1

    def numbers(*values):
        return jnp.stack([v.astype(jnp.int32) for v in values])

    zx = numbers(z, x)
    sources = [
        (chip_z ^ dz) * 8 + ((chip_y - dy * (1 - 2 * c)) & 3) * 2 + c
        for c in (core, 1 - core)
        for dz, dy in CHIPS
    ]
    early = 6
    span_early, span_late = slice(0, early * LANES), slice(early * LANES, 8 * LANES)

    def over_x(blocks):
        return [blocks[0]] + [move_hist(blocks[d], 0, d) for d in (2, 1, 3)]

    def gathered(value):
        mine, theirs = rows[:2], rows[2:]
        own = [value] + [move_tcol(value, dz, dy) for dz, dy in CHIPS[1:6]]
        own += [move_tcol(own[1], 0, 1), move_tcol(own[2], 0, 1)]
        begun, stack = propagate(mine, own[:early], zx, span_early, (), True)
        first = other_core(stack)
        begun, stack = propagate(mine, own[early:], zx, span_late, [begun], True)
        last = other_core(stack)
        return propagate(theirs, [first], zx, span_early, [begun])[0], last

    blocks = collect(history, memory_weight_first, zx, True)
    pairs = over_x(blocks)
    sums = collect(history, memory_weight_second, zx, False, [blocks[0]])[0]
    far, keep = add_pairs(pairs, zx, [sums])
    other_z = move_hist(far, 1, 0)
    near_blocks = cut_sums(sums, zx, [far])
    near_a = move_hist(near_blocks[2], 0, 2)
    near_b = [move_hist(near_blocks[d], 0, d) for d in (1, 3)]
    pred_one, sigma = predict(explicit_first, [keep, other_z], zx, [near_blocks[0]])
    near_blocks = [near_blocks[0], near_a, *near_b]

    rows = split_propagator(propagator, numbers(*sources, x), sums)
    begun, block = gathered(sigma)
    blocks = finish_first(rows[2:], [block], zx, span_late, begun)
    matrices = split_matrices([inverse_one, link, inverse_two], zx, [blocks[0]])
    parts = over_x(blocks)

    near = add_blocks(near_blocks, zx, [blocks[0]])
    near_other = move_hist(near, 1, 0)

    right = right_side(pred_one, parts, zx)
    moved, kept, *pieces = solve(
        right, move_hist(right, 1, 0), matrices, explicit_second, near, near_other, zx
    )
    begun, block = gathered(moved)
    pieces = over_x(pieces)
    blocks = finish_second(rows[2:], [block], zx, span_late, begun, kept)
    return tuple(last_rows(pieces, over_x(blocks), zx))


def solution(mesh):
    return jax.shard_map(
        shards,
        mesh=mesh,
        in_specs=(
            P("hist", "tcol"),
            P(None, "hist"),
            P(None, "hist"),
            P(),
            P(None, "tcol"),
            P(),
            P(),
            P(None, "tcol"),
            P(None, "tcol"),
        ),
        out_specs=(P("hist", "tcol"), P("hist", "tcol")),
        check_vma=False,
    )
```

```python
import jax
import jax.numpy as jnp
from jax import lax
from jax.experimental import pallas as pl
from jax.experimental.pallas import tpu as pltpu
from jax.sharding import PartitionSpec as P


strength = 0.2
step_size = 0.5
F32, BF16 = jnp.float32, jnp.bfloat16
WHOLE = pl.BlockSpec(memory_space=pltpu.VMEM)
SCALARS = pl.BlockSpec(memory_space=pltpu.SMEM)
CHUNKS = (256, 256, 512, 512, 512)
LANES = 128
UNREAD = pl.BlockSpec(memory_space=pl.ANY)

CHIPS = ((0, 0), (0, 1), (1, 1), (1, -1), (0, -1), (1, 0), (0, 2), (1, 2))


def move_hist(value, dz, dx):
    pairs = [(i, ((i >> 2) ^ dz) * 4 + ((i & 3) + dx) % 4) for i in range(8)]
    return lax.ppermute(value, "hist", pairs)


def move_tcol(value, dz, dy):
    def target(i):
        y = ((i >> 1) + (-dy if i & 1 else dy)) % 4
        return ((i >> 3) ^ dz) * 8 + y * 2 + (i & 1)

    return lax.ppermute(value, "tcol", [(i, target(i)) for i in range(16)])


def other_core(value):
    return lax.ppermute(value, "tcol", [(i, i ^ 1) for i in range(16)])


def cubic_power(value):
    return strength * value * value * value


def split(value):
    high = value.astype(BF16)
    return high, (value - high.astype(F32)).astype(BF16)


def product(left, right):
    def dot(a, b):
        return jnp.dot(a, b, preferred_element_type=F32)

    return dot(left[0], right[0]) + (dot(left[0], right[1]) + dot(left[1], right[0]))


def narrow_product(left, right):
    n = right[0].shape[1]
    wide = jnp.dot(left[0], jnp.concatenate(right, axis=1), preferred_element_type=F32)
    low = jnp.dot(left[1], right[0], preferred_element_type=F32)
    return wide[:, :n] + (wide[:, n:] + low)


def total(refs):
    value = refs[0][...]
    for ref in refs[1:]:
        value = value + ref[...]
    return value


def rows_from(start, count):
    return pl.ds(pl.multiple_of(start, count), count)


def call(kernel, outs, where, inputs, after=(), scratch=()):
    n = len(after)

    def body(at, *refs):
        kernel(at, *refs[: len(inputs)], *refs[len(inputs) + n :])

    return pl.pallas_call(
        body,
        in_specs=[SCALARS] + [WHOLE] * len(inputs) + [UNREAD] * n,
        out_shape=[jax.ShapeDtypeStruct(shape, dtype) for shape, dtype in outs],
        out_specs=[WHOLE] * len(outs),
        scratch_shapes=[pltpu.VMEM(shape, F32) for shape in scratch],
        compiler_params=pltpu.CompilerParams(vmem_limit_bytes=8 << 20),
    )(where, *inputs, *after)


def in_hbm(array):
    return pltpu.with_memory_space_constraint(array, pltpu.HBM)


def lanes_from(block):
    return pl.ds(pl.multiple_of(block * LANES, LANES), LANES)


def collect(history, weights, where, cut, after=()):
    depth, cols = history.shape
    rows = weights.shape[0]
    half = rows // 2
    n = len(after)
    ends = [depth * sum(CHUNKS[: r + 1]) // sum(CHUNKS) for r in range(len(CHUNKS))]
    steps = len(ends)
    shapes = [(2, half, LANES)] * 4 if cut else [(rows, cols)]

    def kernel(at, hist_ref, weight_ref, *rest):
        outs = rest[n : n + len(shapes)]
        hist, weight, arrived = rest[n + len(shapes) : n + len(shapes) + 3]
        acc = rest[-1] if cut else outs[0]
        copies = []
        for r in range(steps):
            lines = slice(ends[r - 1] if r else 0, ends[r])
            pair = (
                pltpu.make_async_copy(hist_ref.at[lines, :], hist.at[lines, :], arrived.at[r, 0]),
                pltpu.make_async_copy(
                    weight_ref.at[:, lines], weight.at[:, lines], arrived.at[r, 1]
                ),
            )
            for copy in pair:
                copy.start()
            copies.append((lines, pair))
        for r, (lines, pair) in enumerate(copies):
            for copy in pair:
                copy.wait()
            value = product(split(weight[:, lines]), split(cubic_power(hist[lines, :])))
            acc[...] = value if r == 0 else acc[...] + value
        if cut:
            for near in range(2):
                lines = rows_from((at[0] ^ (1 - near)) * half, half)
                for d in range(4):
                    outs[d][near] = acc[lines, lanes_from((at[1] + d) & 3)]

    scratch = [
        pltpu.VMEM((depth, cols), F32),
        pltpu.VMEM((rows, depth), F32),
        pltpu.SemaphoreType.DMA((steps, 2)),
    ]
    return pl.pallas_call(
        kernel,
        in_specs=[SCALARS, UNREAD, UNREAD] + [UNREAD] * n,
        out_specs=[WHOLE] * len(shapes),
        scratch_shapes=scratch + ([pltpu.VMEM((rows, cols), F32)] if cut else []),
        out_shape=[jax.ShapeDtypeStruct(shape, F32) for shape in shapes],
        name="collect",
        compiler_params=pltpu.CompilerParams(vmem_limit_bytes=20 << 20),
    )(where, in_hbm(history), in_hbm(weights), *after)


def cut_sums(sums, where, after):
    def kernel(at, sums_ref, *outs):
        for d in range(4):
            outs[d][...] = sums_ref[:, lanes_from((at[1] + d) & 3)]

    outs = [((sums.shape[0], LANES), F32)] * 4
    return call(kernel, outs, where, [sums], after)


def split_propagator(propagator, where, after):
    cols = propagator.shape[1]
    blocks = in_hbm(propagator.reshape(16, 4, LANES, cols))

    def kernel(at, blocks_ref, _, *refs):
        outs, held, arrived = refs[:4], refs[4], refs[5]
        copies = [
            pltpu.make_async_copy(blocks_ref.at[at[k], at[16]], held.at[k], arrived.at[k])
            for k in range(16)
        ]
        for copy in copies:
            copy.start()
        for k, copy in enumerate(copies):
            copy.wait()
            lines = slice((k & 7) * LANES, ((k & 7) + 1) * LANES)
            high, low = split(held[k])
            outs[2 * (k >> 3)][lines, :], outs[2 * (k >> 3) + 1][lines, :] = high, low

    return pl.pallas_call(
        kernel,
        in_specs=[SCALARS, UNREAD, UNREAD],
        out_specs=[WHOLE] * 4,
        scratch_shapes=[pltpu.VMEM((16, LANES, cols), F32), pltpu.SemaphoreType.DMA((16,))],
        out_shape=[jax.ShapeDtypeStruct((8 * LANES, cols), BF16)] * 4,
        name="split_propagator",
        compiler_params=pltpu.CompilerParams(vmem_limit_bytes=12 << 20),
    )(where, blocks, after)


def split_matrices(matrices, where, after):
    size = matrices[0].shape[0]
    half = size // 2

    def kernel(at, *refs):
        for n in range(2):
            refs[3 + 2 * n][...], refs[4 + 2 * n][...] = split(refs[n][...])
        refs[7][...], refs[8][...] = split(refs[2][rows_from(at[0] * half, half), :])

    outs = [((size, size), BF16)] * 4 + [((half, size), BF16)] * 2
    return call(kernel, outs, where, matrices, after)


def predict(explicit, parts, where, after):
    half = explicit.shape[0] // 2

    def kernel(at, explicit_ref, *refs):
        pred = explicit_ref[rows_from(at[0] * half, half), lanes_from(at[1])] + total(refs[:-2])
        refs[-2][...] = pred
        refs[-1][...] = cubic_power(pred)

    outs = [((half, LANES), F32)] * 2
    return call(kernel, outs, where, [explicit, *parts], after)


def side_by_side(refs):
    return jnp.concatenate([ref[...] for ref in refs], axis=1)


def times(split_rows, blocks, span):
    return product(split(blocks), (split_rows[0][span, :], split_rows[1][span, :]))


def propagate(split_rows, blocks, where, span, begun=(), stacked=False):
    n = len(blocks)

    def kernel(at, high_ref, low_ref, *refs):
        joined = side_by_side(refs[:n])
        value = times((high_ref, low_ref), joined, span)
        for ref in refs[n : n + len(begun)]:
            value = value + ref[...]
        refs[n + len(begun)][...] = value
        if stacked:
            refs[-1][...] = joined

    rows = blocks[0].shape[0]
    outs = [((rows, split_rows[0].shape[1]), F32)]
    if stacked:
        outs.append(((rows, span.stop - span.start), F32))
    return call(kernel, outs, where, [*split_rows, *blocks, *begun])


def finish_first(split_rows, blocks, where, span, begun):
    n = len(blocks)

    def kernel(at, high_ref, low_ref, *refs):
        acc = refs[-1]
        acc[...] = refs[n][...] + times((high_ref, low_ref), side_by_side(refs[:n]), span)
        for d in range(4):
            refs[n + 1 + d][...] = acc[:, lanes_from((at[1] + d) & 3)]

    rows, cols = begun.shape
    outs = [((rows, LANES), F32)] * 4
    inputs = [*split_rows, *blocks, begun]
    return call(kernel, outs, where, inputs, (), [(rows, cols)])


def finish_second(split_rows, blocks, where, span, begun, kept):
    n = len(blocks)
    rows, cols = begun.shape
    part = rows // 4

    def kernel(at, high_ref, low_ref, *refs):
        outs, acc = refs[n + 2 : -1], refs[-1]
        acc[...] = refs[n][...] + times((high_ref, low_ref), side_by_side(refs[:n]), span)
        mine = lanes_from(at[1])
        acc[:, mine] = acc[:, mine] + refs[n + 1][...]
        for d in range(4):
            outs[d][...] = acc[rows_from(((at[1] + d) & 3) * part, part), :]

    outs = [((part, cols), F32)] * 4
    inputs = [*split_rows, *blocks, begun, kept]
    return call(kernel, outs, where, inputs, (), [(rows, cols)])


def right_side(pred, parts, where):
    def kernel(at, pred_ref, *refs):
        refs[-1][...] = pred_ref[...] + step_size * total(refs[:-1])

    return call(kernel, [(pred.shape, F32)], where, [pred, *parts])[0]


def begin_solve(right_own, matrix, explicit_two, near_own, near_other, where):
    half = right_own.shape[0]

    def kernel(at, own_ref, high_ref, low_ref, explicit_ref, near_ref, far_ref, *outs):
        mine = pl.ds(pl.multiple_of(at[0] * half, half), half)
        matrix = (high_ref[:, mine], low_ref[:, mine])
        outs[0][...] = narrow_product(matrix, split(own_ref[...]))
        outs[1][...] = explicit_ref[:, lanes_from(at[1])] + (near_ref[...] + far_ref[...])

    outs = [((2 * half, LANES), F32)] * 2
    inputs = [right_own, *matrix, explicit_two, near_own, near_other]
    return call(kernel, outs, where, inputs)


def solve(begun, right_other, matrices, base, where):
    half = right_other.shape[0]
    part = half // 4

    def kernel(at, begun_ref, other_ref, base_ref, *rest):
        mats, (moved_ref, kept_ref), pieces, first = rest[:6], rest[6:8], rest[8:12], rest[12]
        far = pl.ds(pl.multiple_of((at[0] ^ 1) * half, half), half)
        matrix = (mats[0][:, far], mats[1][:, far])
        first[...] = begun_ref[...] + narrow_product(matrix, split(other_ref[...]))
        pred = base_ref[...] + narrow_product((mats[2][...], mats[3][...]), split(cubic_power(first[...])))
        both = jnp.concatenate([step_size * cubic_power(pred), pred], axis=1)
        solved = product((mats[4][...], mats[5][...]), split(both))
        moved_ref[...] = solved[:, :LANES]
        kept_ref[...] = solved[:, LANES:]
        for d in range(4):
            pieces[d][...] = first[rows_from((at[0] * 4 + ((at[1] + d) & 3)) * part, part), :]

    outs = [((half, LANES), F32)] * 2 + [((part, LANES), F32)] * 4
    inputs = [begun, right_other, base, *matrices]
    return call(kernel, outs, where, inputs, (), [(2 * half, LANES)])


def add_pairs(blocks, where, after):
    def kernel(at, *refs):
        ins, far_ref, keep_ref = refs[:4], refs[4], refs[5]
        far_ref[...] = (ins[0][0] + ins[1][0]) + (ins[2][0] + ins[3][0])
        keep_ref[...] = (ins[0][1] + ins[1][1]) + (ins[2][1] + ins[3][1])

    return call(kernel, [(blocks[0].shape[1:], F32)] * 2, where, blocks, after)


def add_blocks(blocks, where, after):
    def kernel(at, *refs):
        refs[-1][...] = total(refs[:-1])

    return call(kernel, [(blocks[0].shape, F32)], where, blocks, after)[0]


def last_rows(pieces, parts, where):
    part, cols = parts[0].shape

    def kernel(at, *refs):
        first_ref, second_ref = refs[8], refs[9]
        second_ref[...] = total(refs[4:8])
        for ref, d in zip(refs[:4], (0, 2, 1, 3)):
            first_ref[:, lanes_from((at[1] - d) & 3)] = ref[...]

    outs = [((part, cols), F32)] * 2
    return call(kernel, outs, where, [*pieces, *parts])


def shards(
    history,
    memory_weight_first,
    memory_weight_second,
    link,
    propagator,
    inverse_one,
    inverse_two,
    explicit_first,
    explicit_second,
):
    h = lax.axis_index("hist")
    t = lax.axis_index("tcol")
    z, x = h >> 2, h & 3
    chip_z, chip_y, core = t >> 3, (t >> 1) & 3, t & 1

    def numbers(*values):
        return jnp.stack([v.astype(jnp.int32) for v in values])

    zx = numbers(z, x)
    sources = [
        (chip_z ^ dz) * 8 + ((chip_y - dy * (1 - 2 * c)) & 3) * 2 + c
        for c in (core, 1 - core)
        for dz, dy in CHIPS
    ]
    early = 6
    span_early, span_late = slice(0, early * LANES), slice(early * LANES, 8 * LANES)

    def over_x(blocks):
        return [blocks[0]] + [move_hist(blocks[d], 0, d) for d in (2, 1, 3)]

    def gathered(value):
        mine, theirs = rows[:2], rows[2:]
        own = [value] + [move_tcol(value, dz, dy) for dz, dy in CHIPS[1:6]]
        own += [move_tcol(own[1], 0, 1), move_tcol(own[2], 0, 1)]
        begun, stack = propagate(mine, own[:early], zx, span_early, (), True)
        first = other_core(stack)
        begun, stack = propagate(mine, own[early:], zx, span_late, [begun], True)
        last = other_core(stack)
        return propagate(theirs, [first], zx, span_early, [begun])[0], last

    blocks = collect(history, memory_weight_first, zx, True)
    pairs = over_x(blocks)
    sums = collect(history, memory_weight_second, zx, False, [blocks[0]])[0]
    far, keep = add_pairs(pairs, zx, [sums])
    other_z = move_hist(far, 1, 0)
    near_blocks = cut_sums(sums, zx, [far])
    near_a = move_hist(near_blocks[2], 0, 2)
    near_b = [move_hist(near_blocks[d], 0, d) for d in (1, 3)]
    pred_one, sigma = predict(explicit_first, [keep, other_z], zx, [near_blocks[0]])
    near_blocks = [near_blocks[0], near_a, *near_b]

    rows = split_propagator(propagator, numbers(*sources, x), sums)
    begun, block = gathered(sigma)
    blocks = finish_first(rows[2:], [block], zx, span_late, begun)
    matrices = split_matrices([inverse_one, link, inverse_two], zx, [blocks[0]])
    parts = over_x(blocks)

    near = add_blocks(near_blocks, zx, [blocks[0]])
    near_other = move_hist(near, 1, 0)

    right = right_side(pred_one, parts, zx)
    right_other = move_hist(right, 1, 0)
    begun, base = begin_solve(right, matrices[:2], explicit_second, near, near_other, zx)
    moved, kept, *pieces = solve(begun, right_other, matrices, base, zx)
    begun, block = gathered(moved)
    pieces = over_x(pieces)
    blocks = finish_second(rows[2:], [block], zx, span_late, begun, kept)
    return tuple(last_rows(pieces, over_x(blocks), zx))


def solution(mesh):
    return jax.shard_map(
        shards,
        mesh=mesh,
        in_specs=(
            P("hist", "tcol"),
            P(None, "hist"),
            P(None, "hist"),
            P(),
            P(None, "tcol"),
            P(),
            P(),
            P(None, "tcol"),
            P(None, "tcol"),
        ),
        out_specs=(P("hist", "tcol"), P("hist", "tcol")),
        check_vma=False,
    )
```
